32 devices in a mesh: tile: 8 (over y, x, core), lev: 4 (over z).
Axes of the slice: x: 2, y: 2, z: 4, core: 2. Of those that a mesh axis runs over, the one named last changes fastest.
Arguments:
- control: float32 [20, 128, 96, 128], P(None, 'lev', 'tile'), may hold values from -6 to 6
- ensemble: bfloat16 [20, 128, 96, 128], P(None, 'lev', 'tile'), may hold values from -6 to 6
- coupling_x: float32 [96, 128], P('tile'), may hold values from 0.16 to 0.245
- coupling_y: float32 [128], replicated, may hold values from 0.16 to 0.245
- vertical_loc: bfloat16 [128, 128], replicated
- obs_cells: int32 [64, 32], P('tile'), may hold values from 0 to 1535, as said below
- obs_counts: int32 [64], P('tile'), may hold values from 8 to 32, as said below
- obs_values: float32 [64, 32, 128], P('tile', None, 'lev'), may hold values from -6 to 6
Outputs:
- increment: float32 [128, 96, 128], P('lev', 'tile')
- gradient: float32 [20, 128, 96, 128], P(None, 'lev', 'tile')
The draws below stay inside these ranges and needn't reach their ends.
Inputs may be any that keep to these rules, and one draw needn't show every extreme that they name: `obs_cells`: each row holds owner-local cells of one owner, in rising order. The live slots of a row are its first obs_counts entries; in every draw some owners receive 32 live slots from every device.
All inputs are finite; a program needn't handle non-finite values.
Results may differ from the reference program's by a relative error of at most 0.0029.
Values may be sent and summed in bfloat16 or wider, within the bound.
A program may use at most 64 MiB of HBM per device.

```python
import math
import jax
import jax.numpy as jnp
from jax import lax

M = 20
L = 128
CX = 12
CY = 128
STEPS = 4
CAP = 32
OWNERS = 8
NX = 96
OBS_ROWS = 64


def draw_control(key, part):
    normal_part = jax.random.normal(key, (M, L, NX, CY), jnp.float32)
    return jnp.clip(normal_part, -6.0, 6.0)


def draw_vertical_loc(key, part):
    levels = jnp.arange(L, dtype=jnp.float32)
    distance = (levels[:, None] - levels[None, :]) / (L / 1.5)
    factor = jax.random.uniform(key, (L, L), jnp.float32, 0.5, 1.5)
    return (0.5 * factor * (0.15 + jnp.exp(-distance * distance))).astype(jnp.bfloat16)


def draw_obs_cells(key, part):
    raw_cells = jax.random.randint(key, (OBS_ROWS, CAP), 0, CX * CY, dtype=jnp.int32)
    return jnp.sort(raw_cells, axis=1)


def draw_obs_counts(key, part):
    owner = jnp.arange(OBS_ROWS, dtype=jnp.int32) % OWNERS
    shuffled = jax.random.permutation(jax.random.fold_in(key, 7), OWNERS)
    busiest = shuffled[:max(1, OWNERS // 8)]
    is_busy = jnp.any(owner[:, None] == busiest[None, :], axis=1)
    base_count = jax.random.randint(jax.random.fold_in(key, 3), (OBS_ROWS,), CAP // 4, CAP // 2 + 1, dtype=jnp.int32)
    return jnp.where(is_busy, jnp.int32(CAP), base_count).astype(jnp.int32)


def level_of(own_key, shape, pieces, smallest, high):
    level, own = 1.0, jax.random.fold_in(own_key, 6)
    for dim, blocks in pieces:
        heights = jnp.exp(jax.random.uniform(jax.random.fold_in(own, dim), (blocks,), jnp.float32, smallest / len(pieces), high / len(pieces)))
        level = level * jnp.repeat(heights, shape[dim] // blocks).reshape([-1 if axis == dim else 1 for axis in range(len(shape))])
    return level


def gaussian(key, extent, spread, most, shards=(), kind=jnp.bfloat16):
    result = jax.random.normal(key, extent, jnp.float32) * spread
    if len(shards) > 0:
        result = level_of(key, extent, shards, -0.22, 0.18) * result
    return jnp.clip(result, min=-most, max=most).astype(kind)


def setup_inputs(seed: int = 0) -> dict:
    key_list = jax.random.split(jax.random.key(seed), 9)
    control = draw_control(jax.random.fold_in(key_list[8], 71), 0)
    ensemble = gaussian(key_list[1], (M, L, NX, CY), 1.0, 6.0, ((1, 4), (2, 8)))
    coupling_x = jnp.clip(jnp.exp(math.log(0.245) - 0.42608444 * jax.random.uniform(key_list[2], (NX, CY), jnp.float32) ** level_of(key_list[2], (NX, CY), ((0, 8),), -0.2, 0.2)), 0.16, 0.245)
    coupling_y = jnp.clip(jnp.exp(jax.random.uniform(key_list[3], (CY,), jnp.float32, math.log(0.16), math.log(0.245))), 0.16, 0.245)
    vertical_loc = draw_vertical_loc(jax.random.fold_in(key_list[8], 71), 0)
    obs_cells = draw_obs_cells(jax.random.fold_in(key_list[8], 71), 0)
    obs_counts = draw_obs_counts(jax.random.fold_in(key_list[8], 71), 0)
    obs_values = gaussian(key_list[7], (OBS_ROWS, CAP, L), 1.0, 6.0, ((0, 8), (2, 4)), jnp.float32)
    return dict(control=control, ensemble=ensemble, coupling_x=coupling_x, coupling_y=coupling_y, vertical_loc=vertical_loc, obs_cells=obs_cells, obs_counts=obs_counts, obs_values=obs_values)


def sweep_across(middle, coupling_y):
    differ = middle[..., 1:] - middle[..., :-1]
    fluxes = coupling_y[:-1] * differ
    zeros_col = jnp.zeros_like(middle[..., :1])
    return jnp.concatenate([fluxes, zeros_col], -1) - jnp.concatenate([zeros_col, fluxes], -1)


def diffuse(field, coupling_x, coupling_y):
    behind_x = jnp.roll(coupling_x, 1, 0)
    for step in range(STEPS):
        forward_col = jnp.roll(field, -1, -2)
        backward_col = jnp.roll(field, 1, -2)
        field = field + (coupling_x * (forward_col - field) - behind_x * (field - backward_col)) + sweep_across(field, coupling_y)
    return field


def reference(control, ensemble, coupling_x, coupling_y, vertical_loc, obs_cells, obs_counts, obs_values):
    slot_index = lax.broadcasted_iota(jnp.int32, obs_cells.shape, 1)
    live = slot_index < obs_counts[:, None]
    masked = jnp.where(live[..., None], obs_values, jnp.float32(0.0))
    owner = (jnp.arange(OBS_ROWS, dtype=jnp.int32) % OWNERS).astype(jnp.int32)
    flat_ids = (owner[:, None] * (CX * CY) + obs_cells).astype(jnp.int32)
    summed = jax.ops.segment_sum(masked.reshape(-1, L), flat_ids.reshape(-1), num_segments=NX * CY)
    obs_grad = summed.T.reshape(L, NX, CY)

    def forward_member(carry, pair):
        member_ctl, member_ens = pair
        smooth = diffuse(member_ctl, coupling_x, coupling_y).astype(jnp.bfloat16)
        localized = jnp.dot(vertical_loc, smooth.reshape(L, -1), preferred_element_type=jnp.float32).reshape(L, NX, CY)
        return carry + member_ens.astype(jnp.float32) * localized, None

    increment, unused = lax.scan(forward_member, jnp.zeros((L, NX, CY), jnp.float32), (control, ensemble))

    def adjoint_member(pair):
        member_ctl, member_ens = pair
        weighted = (member_ens.astype(jnp.float32) * obs_grad).astype(jnp.bfloat16)
        returned = jnp.dot(vertical_loc.T, weighted.reshape(L, -1), preferred_element_type=jnp.float32).reshape(L, NX, CY)
        return member_ctl + diffuse(returned, coupling_x, coupling_y)

    gradient = lax.map(adjoint_member, (control, ensemble))
    return increment, gradient
```

```python
import functools

import jax
import jax.numpy as jnp
from jax import lax
from jax.experimental import pallas as pl
from jax.experimental.pallas import tpu as pltpu
from jax.sharding import PartitionSpec as P


STEPS = 4


def shift_by(value, axis, shift):
    size = lax.axis_size(axis)
    return lax.ppermute(value, axis, [(i, (i + shift) % size) for i in range(size)])


def cost(flops, moved):
    return pl.CostEstimate(flops=int(flops), bytes_accessed=int(moved), transcendentals=0)


def diffuse_rows(rows, cx, cy):
    lanes = rows[0].shape[-1]
    for step in range(STEPS):
        flux = [cx[step + i] * (rows[i + 1] - rows[i]) for i in range(len(rows) - 1)]
        fresh = []
        for i in range(1, len(rows) - 1):
            u = rows[i]
            across = cy * (pltpu.roll(u, lanes - 1, 1) - u)
            fresh.append(u + (flux[i] - flux[i - 1]) + (across - pltpu.roll(across, 1, 1)))
        rows = fresh
    return rows


def face_rows(cx_ref, cy_ref):
    count = cx_ref.shape[0]
    cx = [cx_ref[pl.ds(i, 1), :] for i in range(count)]
    cy = cy_ref[...]
    lane = lax.broadcasted_iota(jnp.int32, cy.shape, 1)
    return cx, jnp.where(lane < cy.shape[1] - 1, cy, 0.0)


def by_eights(load, block, cx, cy, store):
    for start in range(0, block, 16):
        whole = load(pl.ds(start, 16))
        halves = [diffuse_rows([row[h : h + 8] for row in whole], cx, cy) for h in (0, 8)]
        for i, pair in enumerate(zip(*halves)):
            store(i, pl.ds(start, 16), jnp.concatenate(pair, axis=0))


def smooth_kernel(me_ref, before_ref, ctl_ref, after_ref, cx_ref, cy_ref, *rest):
    out_ref = rest[-1]
    cx, cy = face_rows(cx_ref, cy_ref)
    columns, block = ctl_ref.shape[1], ctl_ref.shape[2]

    def load(part):
        rows = [before_ref[0, i, part, :].astype(jnp.float32) for i in range(STEPS)]
        rows += [ctl_ref[0, i, part, :] for i in range(columns)]
        return rows + [after_ref[0, i, part, :].astype(jnp.float32) for i in range(STEPS)]

    def store(i, part, row):
        out_ref[0, i, part, :] = row.astype(out_ref.dtype)

    by_eights(load, block, cx, cy, store)


def smooth_of(me, ahead, ctl, before, after, cx_ext, cy, *earlier):
    members, columns, block, across = ctl.shape
    size = lax.axis_size("lev")
    each = members // size
    of_group = lambda m, me: (lax.rem(me[0] + ahead, size) * each + m, 0, 0, 0)
    fixed = lambda m, me: (0, 0)
    halo = pl.BlockSpec((1, STEPS, block, across), of_group)
    shape = (1, columns, block, across)
    return pl.pallas_call(
        smooth_kernel,
        out_shape=jax.ShapeDtypeStruct((each,) + ctl.shape[1:], jnp.bfloat16),
        grid_spec=pltpu.PrefetchScalarGridSpec(
            num_scalar_prefetch=1,
            grid=(each,),
            in_specs=[
                halo,
                pl.BlockSpec(shape, of_group),
                halo,
                pl.BlockSpec(cx_ext.shape, fixed),
                pl.BlockSpec(cy.shape, fixed),
            ]
            + [pl.BlockSpec(memory_space=pl.ANY)] * len(earlier),
            out_specs=pl.BlockSpec(shape, lambda m, me: (m, 0, 0, 0)),
        ),
        cost_estimate=cost(60 * ctl.size // size, 8 * ctl.size // size),
    )(me.reshape(1), before, ctl, after, cx_ext, cy, *earlier)


def pack_kernel(first_ref, last_ref, out_first, out_last):
    out_first[...] = first_ref[...].astype(jnp.bfloat16)
    out_last[...] = last_ref[...].astype(jnp.bfloat16)


def pack_edges(ctl):
    members, columns, block, across = ctl.shape
    step = max(d for d in (1, 2, 4, 5, 10) if members % d == 0)
    shape = (step, STEPS, block, across)
    end = (columns - STEPS) // STEPS
    first = pl.BlockSpec(shape, lambda m: (m, 0, 0, 0))
    last = pl.BlockSpec(shape, lambda m: (m, end, 0, 0))
    out = jax.ShapeDtypeStruct((members,) + shape[1:], jnp.bfloat16)
    return pl.pallas_call(
        pack_kernel,
        grid=(members // step,),
        out_shape=[out, out],
        in_specs=[first, last],
        out_specs=[first, first],
        cost_estimate=cost(ctl.size, 4 * ctl.size),
    )(ctl, ctl)


def gradient_kernel(me_ref, low_ref, own_ref, high_ref, ctl_ref, cx_ref, cy_ref, late_ref, out_ref, field):
    columns, block, across = ctl_ref.shape[1:]
    members = field.shape[1]

    @pl.when(pl.program_id(0) == 0)
    def _():
        spots = lax.broadcasted_iota(jnp.int32, (across, own_ref.shape[2]), 0)

        def spread(ref, column, place):
            spot = ref[members, 0:2, :].astype(jnp.float32).astype(jnp.int32)
            cell = spot[0:1] * across + spot[1:2]
            chosen = (cell == spots + column * across).astype(jnp.float32).astype(jnp.bfloat16)
            values = ref[0:members].reshape(members * block, -1)
            dense = lax.dot_general(
                values, chosen, (((1,), (1,)), ((), ())), preferred_element_type=jnp.float32
            )
            field[place] = dense.reshape(members, block, across)

        for i in range(STEPS):
            spread(low_ref, columns - STEPS + i, i)
        for i in range(columns):
            spread(own_ref, i, STEPS + i)
        for i in range(STEPS):
            spread(high_ref, i, STEPS + columns + i)

    cx, cy = face_rows(cx_ref, cy_ref)
    member = pl.program_id(0)

    def load(part):
        return [field[i, member, part, :] for i in range(columns + 2 * STEPS)]

    def store(i, part, row):
        out_ref[0, i, part, :] = ctl_ref[0, i, part, :] + row

    by_eights(load, block, cx, cy, store)


def gradient_of(me, ctl, low, own, high, cx_ext, cy, late):
    members, columns, block, across = ctl.shape
    size = lax.axis_size("lev")
    each = members // size

    def placed(m, me):
        return (lax.rem(me[0] + m // each, size) * each + lax.rem(m, each), 0, 0, 0)

    main = pl.BlockSpec((1, columns, block, across), placed)
    whole = lambda a: pl.BlockSpec(a.shape, lambda m, me: (0,) * a.ndim)
    return pl.pallas_call(
        gradient_kernel,
        out_shape=jax.ShapeDtypeStruct(ctl.shape, jnp.float32),
        grid_spec=pltpu.PrefetchScalarGridSpec(
            num_scalar_prefetch=1,
            grid=(members,),
            in_specs=[whole(low), whole(own), whole(high), main, whole(cx_ext), whole(cy)]
            + [pl.BlockSpec(memory_space=pl.ANY)],
            out_specs=main,
            scratch_shapes=[
                pltpu.VMEM((columns + 2 * STEPS, members, block, across), jnp.float32)
            ],
        ),
        cost_estimate=cost(100 * ctl.size, 10 * ctl.size),
    )(me.reshape(1), low, own, high, ctl, cx_ext, cy, late)


def weigh_kernel(ens_ref, row_ref, col_ref, vals_ref, out_ref, first_ref):
    members, columns, block, across = ens_ref.shape
    slots = row_ref.shape[1]
    row = row_ref[...]
    same = row == col_ref[...]
    summed = jnp.dot(
        vals_ref[...],
        same.astype(jnp.float32),
        precision=lax.Precision.HIGHEST,
        preferred_element_type=jnp.float32,
    )
    earlier = lax.broadcasted_iota(jnp.int32, (slots, slots), 0) < lax.broadcasted_iota(
        jnp.int32, (slots, slots), 1
    )
    repeats = jnp.sum(jnp.where(same & earlier, 1.0, 0.0), axis=0, keepdims=True)
    column = row // across
    line = lax.broadcasted_iota(jnp.int32, (block, slots), 0)
    place = jnp.where(line == 0, jnp.where(repeats > 0.5, -1, column), row - column * across)
    first_ref[0] = place.astype(jnp.float32).astype(jnp.bfloat16)
    spots = lax.broadcasted_iota(jnp.int32, (across, slots), 0)
    total = jnp.zeros((members * block, slots), jnp.float32)
    for i in range(columns):
        chosen = (row == spots + i * across).astype(jnp.float32).astype(jnp.bfloat16)
        picked = ens_ref[:, i].reshape(members * block, across)
        total += jnp.dot(picked, chosen, preferred_element_type=jnp.float32)
    weighted = total.reshape(members, block, slots) * summed[None]
    out_ref[...] = weighted.astype(jnp.bfloat16)


def weigh(ens, cells, vals):
    members, _, block, _ = ens.shape
    slots = cells.shape[0]
    return pl.pallas_call(
        weigh_kernel,
        out_shape=(
            jax.ShapeDtypeStruct((members, block, slots), jnp.bfloat16),
            jax.ShapeDtypeStruct((1, block, slots), jnp.bfloat16),
        ),
        cost_estimate=cost(2 * slots * ens.size, 2 * ens.size),
    )(ens, cells.reshape(1, slots), cells.reshape(slots, 1), vals.T)


def mix_kernel(count, v_ref, *refs):
    ins, outs = refs[:count], refs[-count:]
    extra, block, width = ins[0].shape[1:]
    pack = max(1, 256 // width)
    matrix = v_ref[...]
    for start in range(0, extra, pack):
        stop = min(start + pack, extra)
        stacked = [jnp.concatenate([r[0, i] for r in ins], axis=0) for i in range(start, stop)]
        right = stacked[0] if len(stacked) == 1 else jnp.concatenate(stacked, axis=1)
        mixed = jnp.dot(matrix, right, preferred_element_type=jnp.float32).astype(jnp.bfloat16)
        for i in range(start, stop):
            lanes = slice((i - start) * width, (i - start + 1) * width)
            for j, out in enumerate(outs):
                out[0, i] = mixed[j * block : (j + 1) * block, lanes]


def mix(matrix, parts, *earlier):
    count = len(parts)
    shape = parts[0].shape
    spec = pl.BlockSpec((1,) + shape[1:], lambda m: (m, 0, 0, 0))
    return pl.pallas_call(
        functools.partial(mix_kernel, count),
        grid=(shape[0],),
        out_shape=[jax.ShapeDtypeStruct(shape, jnp.bfloat16)] * count,
        in_specs=[pl.BlockSpec(matrix.shape, lambda m: (0, 0))]
        + [spec] * count
        + [pl.BlockSpec(memory_space=pl.ANY)] * len(earlier),
        out_specs=[spec] * count,
        cost_estimate=cost(2 * matrix.shape[0] * count * parts[0].size, 4 * count * parts[0].size),
    )(matrix, *parts, *earlier)


def weighted_sum_kernel(count, v_ref, *refs):
    ins, weights, outs, total = refs[:count], refs[count : 2 * count], refs[-count - 1 : -1], refs[-1]
    extra, block, width = ins[0].shape[1:]
    pack = max(1, 256 // width)
    matrix = v_ref[...]
    member = pl.program_id(0)

    @pl.when(member == 0)
    def _():
        total[...] = jnp.zeros_like(total)

    for start in range(0, extra, pack):
        stop = min(start + pack, extra)
        stacked = [jnp.concatenate([r[0, i] for r in ins], axis=0) for i in range(start, stop)]
        right = stacked[0] if len(stacked) == 1 else jnp.concatenate(stacked, axis=1)
        mixed = jnp.dot(matrix, right, preferred_element_type=jnp.float32)
        for i in range(start, stop):
            lanes = slice((i - start) * width, (i - start + 1) * width)
            for j in range(count):
                piece = mixed[j * block : (j + 1) * block, lanes]
                total[j, i] += weights[j][0, i].astype(jnp.float32) * piece

    @pl.when(member == pl.num_programs(0) - 1)
    def _():
        for j, out in enumerate(outs):
            out[...] = total[j].astype(out.dtype)


def weighted_sum(matrix, parts, weights, *earlier):
    count = len(parts)
    shape = parts[0].shape
    spec = pl.BlockSpec((1,) + shape[1:], lambda m: (m, 0, 0, 0))
    done = pl.BlockSpec(shape[1:], lambda m: (0, 0, 0))
    kinds = [jnp.float32] + [jnp.bfloat16] * (count - 1)
    return pl.pallas_call(
        functools.partial(weighted_sum_kernel, count),
        grid=(shape[0],),
        out_shape=[jax.ShapeDtypeStruct(shape[1:], kind) for kind in kinds],
        in_specs=[pl.BlockSpec(matrix.shape, lambda m: (0, 0))]
        + [spec] * (2 * count)
        + [pl.BlockSpec(memory_space=pl.ANY)] * len(earlier),
        out_specs=[done] * count,
        scratch_shapes=[pltpu.VMEM((count,) + shape[1:], jnp.float32)],
        cost_estimate=cost(2 * matrix.shape[0] * count * parts[0].size, 4 * count * parts[0].size),
    )(matrix, *parts, *weights, *earlier)


def groups_of(field, me):
    size = lax.axis_size("lev")
    grouped = field.reshape((size, field.shape[0] // size) + field.shape[1:])
    pick = lambda s: lax.dynamic_index_in_dim(grouped, lax.rem(me + s, size), 0, keepdims=False)
    return [pick(s) for s in range(size)]


def gather_levels(parts):
    return [shift_by(part, "lev", s) if s else part for s, part in enumerate(parts)]


def return_levels(parts):
    return [shift_by(part, "lev", -r) if r else part for r, part in enumerate(parts)]


def dense_returned(ens, obs_values, obs_cells, vert, me):
    _, columns, block, across = ens.shape
    summed = jax.ops.segment_sum(obs_values, obs_cells, num_segments=columns * across)
    obs_grad = summed.T.reshape(block, columns, across).transpose(1, 0, 2)
    weighted = (ens.astype(jnp.float32) * obs_grad[None]).astype(jnp.bfloat16)
    mixed = mix(vert, gather_levels(groups_of(weighted, me)))
    return in_order(return_levels(mixed), me)


def in_order(parts, me):
    size = len(parts)
    stacked = jnp.stack(parts + parts)
    start = lax.rem(size - me, size)
    ordered = lax.dynamic_slice_in_dim(stacked, start, size, 0)
    return ordered.reshape((-1,) + parts[0].shape[1:])


def mega_kernel(
    ctl, ens, cx_own, cy_ref, v_ref, cells, counts, vals, inc, grad,
    edges, halo, cx_halo, masked, got_cells, got_vals, spots_own, spots_halo,
    v_turned, fields, locals_out, locals_in, picked, ret, ret_out, ret_halo, field,
    edge_s, edge_r, cx_s, cx_r, cell_s, cell_r, val_s, val_r, spot_s, spot_r,
    field_s, field_r, loc_s, loc_r, pick_s, pick_r, ret_s, ret_r, low_s, low_r,
):
    members, columns, block, across = ctl.shape
    size, tiles = lax.axis_size("lev"), lax.axis_size("tile")
    owners, cap = cells.shape
    slots = owners * cap
    me, tile = lax.axis_index("lev"), lax.axis_index("tile")
    left, right = lax.rem(tile + tiles - 1, tiles), lax.rem(tile + 1, tiles)
    half = size // 2
    far = jnp.where(me < half, half, half - 1)
    near = jnp.where(me < half, half - 1, half)
    edge = jnp.where(me < half, 0, size - 1)
    inner = me == near
    outer = me != near
    groups = edge_s.shape[1]
    step = members // groups
    parts = pick_s.shape[1]
    share = members // parts

    def to_lev(src, dst, send, recv, lev):
        return pltpu.make_async_remote_copy(
            src_ref=src, dst_ref=dst, send_sem=send, recv_sem=recv,
            device_id={"lev": lev}, device_id_type=pl.DeviceIdType.MESH,
        )

    def to_tile(src, dst, send, recv, where):
        return pltpu.make_async_remote_copy(
            src_ref=src, dst_ref=dst, send_sem=send, recv_sem=recv,
            device_id={"tile": where}, device_id_type=pl.DeviceIdType.MESH,
        )

    def span(first, last, body):
        def wrapped(i, carry):
            body(i)
            return carry

        lax.fori_loop(first, last, wrapped, 0)

    def loop(count, body):
        span(0, count, body)

    barrier = pltpu.get_barrier_semaphore()
    for d in range(1, size):
        pl.semaphore_signal(
            barrier, inc=1, device_id={"lev": lax.rem(me + d, size)},
            device_id_type=pl.DeviceIdType.MESH,
        )
    for d in range(1, tiles):
        pl.semaphore_signal(
            barrier, inc=1, device_id={"tile": lax.rem(tile + d, tiles)},
            device_id_type=pl.DeviceIdType.MESH,
        )

    lane = lax.broadcasted_iota(jnp.int32, (1, cap), 1)
    for r in range(owners):
        masked[r] = jnp.where(lane < counts[r], cells[r : r + 1, :], -1)
    got_cells[tile] = masked[tile]
    got_vals[tile] = vals[tile]

    def pack(g):
        part = pl.ds(g * step, step)
        edges[0, part] = ctl[part, columns - STEPS :].astype(jnp.bfloat16)
        edges[1, part] = ctl[part, :STEPS].astype(jnp.bfloat16)

    def edge_copy(way, g):
        part = pl.ds(g * step, step)
        return to_tile(
            edges.at[way, part], halo.at[way, part], edge_s.at[way, g], edge_r.at[way, g],
            right if way == 0 else left,
        )

    def send_edges(g):
        edge_copy(0, g).start()
        edge_copy(1, g).start()

    pack(0)
    pack(1)
    pl.semaphore_wait(barrier, size + tiles - 2)

    def cx_copy(way):
        return to_tile(
            cx_own, cx_halo.at[way], cx_s.at[way], cx_r.at[way], right if way == 0 else left
        )

    cx_copy(0).start()
    cx_copy(1).start()
    send_edges(0)

    def cell_copy(d):
        where = lax.rem(tile + d, tiles)
        return to_tile(
            masked.at[where], got_cells.at[tile], cell_s.at[d], cell_r.at[tile], where
        )

    def val_copy(d):
        where = lax.rem(tile + d, tiles)
        return to_tile(vals.at[where], got_vals.at[tile], val_s.at[d], val_r.at[tile], where)

    def from_tile(d):
        where = lax.rem(tile + d, tiles)
        to_tile(masked.at[where], got_cells.at[where], cell_s.at[d], cell_r.at[where], where).wait_recv()
        to_tile(vals.at[where], got_vals.at[where], val_s.at[d], val_r.at[where], where).wait_recv()

    for d in range(1, tiles):
        cell_copy(d).start()
        val_copy(d).start()

    def pack_more(g):
        pack(g)
        send_edges(g - 1)

    span(2, groups, pack_more)
    send_edges(groups - 1)

    turned = jnp.transpose(v_ref[...].astype(jnp.float32)).astype(jnp.bfloat16)
    v_turned[...] = turned

    for way in (0, 1):
        cx_copy(way).wait_recv()

    cx = [cx_halo[0, pl.ds(columns - STEPS + i, 1), :] for i in range(STEPS)]
    cx += [cx_own[pl.ds(i, 1), :] for i in range(columns)]
    cx += [cx_halo[1, pl.ds(i, 1), :] for i in range(STEPS)]
    cy = cy_ref[...]
    cy_lane = lax.broadcasted_iota(jnp.int32, cy.shape, 1)
    cy = jnp.where(cy_lane < across - 1, cy, 0.0)

    def smooth(m):
        def load(part):
            rows = [halo[0, m, i, part, :].astype(jnp.float32) for i in range(STEPS)]
            rows += [ctl[m, i, part, :] for i in range(columns)]
            return rows + [halo[1, m, i, part, :].astype(jnp.float32) for i in range(STEPS)]

        def store(i, part, row):
            fields[me, m, i, part, :] = row.astype(jnp.bfloat16)

        by_eights(load, block, cx, cy, store)

    def field_copy(way, m):
        return to_lev(
            fields.at[me, m], fields.at[me, m], field_s.at[way, m], field_r.at[me, m],
            far if way == 0 else near,
        )

    def send_field(m):
        field_copy(0, m).start()

        @pl.when(outer)
        def _():
            field_copy(1, m).start()

    def smooth_step(m):
        @pl.when(lax.rem(m, step) == 0)
        def _():
            g = m // step
            edge_copy(0, g).wait_recv()
            edge_copy(1, g).wait_recv()

        smooth(m)

        @pl.when(m > 0)
        def _():
            send_field(m - 1)

    early = min(3, members)
    span(0, early, smooth_step)

    for d in range(1, tiles):
        from_tile(d)
    row = jnp.concatenate([got_cells[r] for r in range(owners)], axis=1)
    col = jnp.transpose(jnp.broadcast_to(row, (across, slots)).astype(jnp.float32))
    col = jnp.concatenate([col] * (slots // across), axis=1) if slots > across else col[:, :slots]
    same = row.astype(jnp.float32) == col
    values = jnp.concatenate([got_vals[r] for r in range(owners)], axis=0)
    summed = lax.dot_general(
        values,
        same.astype(jnp.float32),
        (((0,), (0,)), ((), ())),
        precision=lax.Precision.HIGHEST,
        preferred_element_type=jnp.float32,
    )
    earlier = lax.broadcasted_iota(jnp.int32, (slots, slots), 0) < lax.broadcasted_iota(
        jnp.int32, (slots, slots), 1
    )
    repeats = jnp.sum(jnp.where(same & earlier, 1.0, 0.0), axis=0, keepdims=True)
    spots_own[...] = jnp.where(repeats > 0.5, -1, row)
    places = lax.broadcasted_iota(jnp.int32, (across, slots), 0)

    def weigh_part(p):
        part = pl.ds(p * share, share)
        total = jnp.zeros((share * block, slots), jnp.float32)
        for i in range(columns):
            chosen = (row == places + i * across).astype(jnp.float32).astype(jnp.bfloat16)
            lines = ens[part, i].reshape(share * block, across)
            total += jnp.dot(lines, chosen, preferred_element_type=jnp.float32)
        weighted = total.reshape(share, block, slots) * summed[None]
        picked[me, part] = weighted.astype(jnp.bfloat16)

    def pick_copy(way, p):
        part = pl.ds(p * share, share)
        return to_lev(
            picked.at[me, part], picked.at[me, part], pick_s.at[way, p], pick_r.at[me, p],
            far if way == 0 else near,
        )

    def send_picked(p):
        pick_copy(0, p).start()

        @pl.when(outer)
        def _():
            pick_copy(1, p).start()

    def weigh_step(p):
        weigh_part(p)

        @pl.when(p > 0)
        def _():
            send_picked(p - 1)

    loop(parts, weigh_step)

    def spot_copy(way):
        return to_tile(
            spots_own, spots_halo.at[way], spot_s.at[way], spot_r.at[way],
            right if way == 0 else left,
        )

    spot_copy(0).start()
    spot_copy(1).start()
    send_picked(parts - 1)

    span(early, members, smooth_step)
    send_field(members - 1)

    def rows_of(ref, at):
        return ref[pl.ds(pl.multiple_of(at * block, block), block), :]

    def ret_copy(p):
        part = pl.ds(p * share, share)
        return to_lev(ret_out.at[part], ret.at[part], ret_s.at[p], ret_r.at[p], edge)

    def ret_wait(p):
        part = pl.ds(p * share, share)
        to_lev(ret_out.at[part], ret.at[part], ret_s.at[p], ret_r.at[p], near).wait_recv()

    def low_copy(way, p):
        part = pl.ds(p * share, share)
        return to_tile(
            ret.at[part], ret_halo.at[way, part], low_s.at[way, p], low_r.at[way, p],
            right if way == 0 else left,
        )

    def send_ret(p):
        low_copy(0, p).start()
        low_copy(1, p).start()

    @pl.when(inner)
    def _():
        both = jnp.concatenate([rows_of(v_turned, me), rows_of(v_turned, edge)], axis=0)

        def mix_step(p):
            for s in range(size):
                @pl.when(me != s)
                def _():
                    part = pl.ds(p * share, share)
                    to_lev(
                        picked.at[s, part], picked.at[s, part], pick_s.at[0, p],
                        pick_r.at[s, p], far,
                    ).wait_recv()

            def one(m):
                stacked = jnp.concatenate([picked[s, m] for s in range(size)], axis=0)
                mixed = jnp.dot(both, stacked, preferred_element_type=jnp.float32)
                mixed = mixed.astype(jnp.bfloat16)
                ret[m] = mixed[:block]
                ret_out[m] = mixed[block:]

            span(p * share, (p + 1) * share, one)
            ret_copy(p).start()
            send_ret(p)

        loop(parts, mix_step)

    inc[...] = jnp.zeros_like(inc)

    def loc_copy(m):
        return to_lev(locals_out.at[m], locals_in.at[m], loc_s.at[m], loc_r.at[m], edge)

    def localize(m):
        both = jnp.concatenate([rows_of(v_ref, me), rows_of(v_ref, edge)], axis=0)
        for s in range(size):
            @pl.when(me != s)
            def _():
                to_lev(
                    fields.at[s, m], fields.at[s, m], field_s.at[0, m], field_r.at[s, m], far
                ).wait_recv()

        for start in range(0, columns, 2):
            some = range(start, min(start + 2, columns))
            stacked = jnp.concatenate(
                [jnp.concatenate([fields[s, m, i] for s in range(size)], axis=0) for i in some],
                axis=1,
            )
            mixed = jnp.dot(both, stacked, preferred_element_type=jnp.float32)
            for j, i in enumerate(some):
                piece = mixed[:, j * across : (j + 1) * across]
                locals_out[m, i] = piece[block:].astype(jnp.bfloat16)
                inc[i] += ens[m, i].astype(jnp.float32) * piece[:block]

        loc_copy(m).start()

    ahead = min(5, members)

    @pl.when(inner)
    def _():
        span(0, ahead, localize)

    @pl.when(outer)
    def _():
        def forward(p):
            ret_wait(p)
            send_ret(p)

        loop(parts, forward)

    for way in (0, 1):
        spot_copy(way).wait_recv()

    def spread(values, cell, column):
        chosen = (cell == places + column * across).astype(jnp.float32).astype(jnp.bfloat16)
        dense = lax.dot_general(
            values, chosen, (((1,), (1,)), ((), ())), preferred_element_type=jnp.float32
        )
        return dense.reshape(share, block, across)

    def spread_part(p):
        low_copy(0, p).wait_recv()
        low_copy(1, p).wait_recv()
        part = pl.ds(p * share, share)
        low = ret_halo[0, part].reshape(share * block, slots)
        own = ret[part].reshape(share * block, slots)
        high = ret_halo[1, part].reshape(share * block, slots)
        for i in range(STEPS):
            field[i, part] = spread(low, spots_halo[0], columns - STEPS + i)
        for i in range(columns):
            field[STEPS + i, part] = spread(own, spots_own[...], i)
        for i in range(STEPS):
            field[STEPS + columns + i, part] = spread(high, spots_halo[1], i)

    def gradient(m):
        def load(part):
            return [field[i, m, part, :] for i in range(columns + 2 * STEPS)]

        def store(i, part, row):
            grad[m, i, part, :] = ctl[m, i, part, :] + row

        by_eights(load, block, cx, cy, store)

    def gradient_part(p):
        spread_part(p)
        span(p * share, (p + 1) * share, gradient)

    loop(parts, gradient_part)

    @pl.when(inner)
    def _():
        span(ahead, members, localize)

    @pl.when(outer)
    def _():
        def add_local(m):
            to_lev(locals_out.at[m], locals_in.at[m], loc_s.at[m], loc_r.at[m], near).wait_recv()
            inc[...] += ens[m].astype(jnp.float32) * locals_in[m].astype(jnp.float32)

        loop(members, add_local)

    for way in (0, 1):
        cx_copy(way).wait_send()
        spot_copy(way).wait_send()
        loop(groups, lambda g: edge_copy(way, g).wait_send())
        loop(parts, lambda p: low_copy(way, p).wait_send())
    for d in range(1, tiles):
        cell_copy(d).wait_send()
        val_copy(d).wait_send()
    loop(members, lambda m: field_copy(0, m).wait_send())
    loop(parts, lambda p: pick_copy(0, p).wait_send())

    @pl.when(outer)
    def _():
        loop(members, lambda m: field_copy(1, m).wait_send())
        loop(parts, lambda p: pick_copy(1, p).wait_send())

    @pl.when(inner)
    def _():
        loop(members, lambda m: loc_copy(m).wait_send())
        loop(parts, lambda p: ret_copy(p).wait_send())


def mega(ctl, ens, cx, cy, vert, cells, counts, vals):
    members, columns, block, across = ctl.shape
    size, tiles = lax.axis_size("lev"), lax.axis_size("tile")
    owners, cap = cells.shape
    slots = owners * cap
    groups = max(d for d in range(1, members + 1) if members % d == 0 and 2 * d <= members)
    parts = max(d for d in range(1, 5) if members % d == 0)
    f32, bf16, i32 = jnp.float32, jnp.bfloat16, jnp.int32
    vmem = pl.BlockSpec(memory_space=pltpu.VMEM)
    smem = pl.BlockSpec(memory_space=pltpu.SMEM)
    dma = lambda *shape: pltpu.SemaphoreType.DMA(shape)
    return pl.pallas_call(
        mega_kernel,
        out_shape=(
            jax.ShapeDtypeStruct(ctl.shape[1:], f32),
            jax.ShapeDtypeStruct(ctl.shape, f32),
        ),
        in_specs=[vmem] * 6 + [smem, vmem],
        out_specs=(vmem, vmem),
        scratch_shapes=[
            pltpu.VMEM((2, members, STEPS, block, across), bf16),
            pltpu.VMEM((2, members, STEPS, block, across), bf16),
            pltpu.VMEM((2,) + cx.shape, f32),
            pltpu.VMEM((owners, 1, cap), i32),
            pltpu.VMEM((owners, 1, cap), i32),
            pltpu.VMEM(vals.shape, f32),
            pltpu.VMEM((1, slots), i32),
            pltpu.VMEM((2, 1, slots), i32),
            pltpu.VMEM(vert.shape, bf16),
            pltpu.VMEM((size,) + ctl.shape, bf16),
            pltpu.VMEM(ctl.shape, bf16),
            pltpu.VMEM(ctl.shape, bf16),
            pltpu.VMEM((size, members, block, slots), bf16),
            pltpu.VMEM((members, block, slots), bf16),
            pltpu.VMEM((members, block, slots), bf16),
            pltpu.VMEM((2, members, block, slots), bf16),
            pltpu.VMEM((columns + 2 * STEPS, members, block, across), f32),
            dma(2, groups), dma(2, groups), dma(2), dma(2),
            dma(tiles), dma(tiles), dma(tiles), dma(tiles), dma(2), dma(2),
            dma(2, members), dma(size, members), dma(members), dma(members),
            dma(2, parts), dma(size, parts), dma(parts), dma(parts),
            dma(2, parts), dma(2, parts),
        ],
        compiler_params=pltpu.CompilerParams(collective_id=0, has_side_effects=True),
    )(ctl, ens, cx, cy, vert, cells, counts, vals)


def local(
    control, ensemble, coupling_x, coupling_y, vertical_loc, obs_cells, obs_counts, obs_values
):
    members, block, columns, across = control.shape
    size = lax.axis_size("lev")
    me = lax.axis_index("lev")
    ctl = control.transpose(0, 2, 1, 3)
    ens = ensemble.transpose(0, 2, 1, 3)
    cy = coupling_y.reshape(1, across)

    rows, cap = obs_cells.shape
    slots = rows * cap
    compact = 2 * slots <= columns * across and slots % across == 0
    if compact and size == 4 and columns >= STEPS and members >= 4 and members % 2 == 0:
        increment, gradient = mega(
            ctl, ens, coupling_x, cy, vertical_loc, obs_cells, obs_counts, obs_values
        )
        return increment.transpose(1, 0, 2), gradient.transpose(0, 2, 1, 3)

    if columns % STEPS == 0:
        first_edge, last_edge = pack_edges(ctl)
    else:
        first_edge = ctl[:, :STEPS].astype(jnp.bfloat16)
        last_edge = ctl[:, columns - STEPS :].astype(jnp.bfloat16)
    first_edge, last_edge, coupling_x, obs_values = lax.optimization_barrier(
        (first_edge, last_edge, coupling_x, obs_values)
    )
    before = shift_by(last_edge, "tile", 1)
    after = shift_by(first_edge, "tile", -1)
    turn = sorted(range(size), key=lambda s: -min(s, size - s))
    ens_sent = groups_of(ens, me)
    for s in range(1, size):
        ens_sent[s] = shift_by(ens_sent[s], "lev", s)
    cx_before = shift_by(coupling_x[columns - STEPS :], "tile", 1)
    cx_after = shift_by(coupling_x[:STEPS], "tile", -1)
    cx_ext = jnp.concatenate([cx_before, coupling_x, cx_after], axis=0)

    level = jnp.arange(block * size, dtype=jnp.int32)
    source = lax.rem(me - level // block + size, size) * block + lax.rem(level, block)
    order = (source[:, None] == level[None, :]).astype(jnp.bfloat16)
    turned = jnp.dot(order, vertical_loc).astype(jnp.bfloat16)
    matrix = jnp.dot(turned, order.T).astype(jnp.bfloat16)

    slot_index = lax.broadcasted_iota(jnp.int32, obs_cells.shape, 1)
    live = slot_index < obs_counts[:, None]
    masked = jnp.where(live[..., None], obs_values, jnp.float32(0.0))
    rows, cap = obs_cells.shape
    payload = jnp.concatenate(
        [masked.reshape(rows, cap * block), obs_cells.astype(jnp.float32)], axis=1
    )
    got = lax.all_to_all(payload, "tile", split_axis=0, concat_axis=0, tiled=True)
    slots = rows * cap
    got_values = got[:, : cap * block].reshape(slots, block)
    got_cells = got[:, cap * block :].astype(jnp.int32).reshape(slots)

    compact = 2 * slots <= columns * across and max(columns, across) <= 256
    if compact:
        weighted, spots = weigh(ens, got_cells, got_values)
        adjoint = gather_levels(groups_of(weighted[:, None], me))

    smooth, earlier = [None] * size, ()
    for rank, s in enumerate(turn):
        smooth[s] = smooth_of(me, s, ctl, before, after, cx_ext, cy, *earlier)
        earlier = (smooth[s],)
        if compact and rank == 0:
            mixed = mix(matrix.T, adjoint, *earlier)
            earlier = (mixed[0],)
            returned = return_levels(mixed)
            back = [part[:, 0] for part in returned]
            own = jnp.concatenate(back + [spots], axis=0)
            low, high = shift_by(own, "tile", 1), shift_by(own, "tile", -1)
    if compact:
        gradient = gradient_of(me, ctl, low, own, high, cx_ext, cy, smooth[0])
        earlier = (gradient,)
    fields = gather_levels(smooth)
    sums = weighted_sum(matrix, fields, ens_sent, *earlier)
    increment = functools.reduce(jnp.add, [p.astype(jnp.float32) for p in return_levels(sums)])

    if not compact:
        returned = dense_returned(ens, got_values, got_cells, matrix.T, me)
        low = shift_by(returned[:, columns - STEPS :], "tile", 1)
        high = shift_by(returned[:, :STEPS], "tile", -1)
        gradient = dense_gradient_of(ctl, returned, low, high, cx_ext, cy)
    return increment.transpose(1, 0, 2), gradient.transpose(0, 2, 1, 3)


def dense_gradient_kernel(low_ref, own_ref, high_ref, ctl_ref, cx_ref, cy_ref, out_ref):
    cx, cy = face_rows(cx_ref, cy_ref)
    columns, block = ctl_ref.shape[1], ctl_ref.shape[2]

    def load(part):
        rows = [low_ref[0, i, part, :].astype(jnp.float32) for i in range(STEPS)]
        rows += [own_ref[0, i, part, :].astype(jnp.float32) for i in range(columns)]
        return rows + [high_ref[0, i, part, :].astype(jnp.float32) for i in range(STEPS)]

    def store(i, part, row):
        out_ref[0, i, part, :] = ctl_ref[0, i, part, :] + row

    by_eights(load, block, cx, cy, store)


def dense_gradient_of(ctl, own, low, high, cx_ext, cy):
    members, columns, block, across = ctl.shape
    halo = pl.BlockSpec((1, STEPS, block, across), lambda m: (m, 0, 0, 0))
    main = pl.BlockSpec((1, columns, block, across), lambda m: (m, 0, 0, 0))
    fixed = lambda m: (0, 0)
    return pl.pallas_call(
        dense_gradient_kernel,
        grid=(members,),
        out_shape=jax.ShapeDtypeStruct(ctl.shape, jnp.float32),
        in_specs=[halo, main, halo, main, pl.BlockSpec(cx_ext.shape, fixed), pl.BlockSpec(cy.shape, fixed)],
        out_specs=main,
        cost_estimate=cost(60 * ctl.size, 12 * ctl.size),
    )(low, own, high, ctl, cx_ext, cy)


def solution(mesh):
    placed = (
        P(None, "lev", "tile", None),
        P(None, "lev", "tile", None),
        P("tile", None),
        P(),
        P(),
        P("tile", None),
        P("tile"),
        P("tile", None, "lev"),
    )

    return jax.shard_map(
        local,
        mesh=mesh,
        in_specs=placed,
        out_specs=(P("lev", "tile", None), P(None, "lev", "tile", None)),
        check_vma=False,
    )
```
